32 devices in a mesh: grp: 2 (over x), mem: 16 (over z, y, core).
Axes of the slice: x: 2, y: 2, z: 4, core: 2. Of those that a mesh axis runs over, the one named last changes fastest.
Arguments:
- field: bfloat16 [128, 16, 64, 256], P(('grp', 'mem')), parts along dimension 0, may hold values from -8 to 8
- norm_gain: float32 [2, 2, 256], replicated, may hold values from 0.1 to 1.9
- conv_weight: bfloat16 [2, 3, 3, 256, 512], replicated, may hold values from -0.125 to 0.125
- qkv_weight: bfloat16 [2, 256, 768], replicated, may hold values from -8 to 8
- out_weight: bfloat16 [2, 256, 256], replicated, may hold values from -0.375 to 0.375
Outputs:
- result: bfloat16 [128, 16, 64, 256], P(('grp', 'mem')), parts along dimension 0
The draws below stay inside these ranges and needn't reach their ends.
There are 2 independent parts, one for each index of `grp`. The reference program is written for one: setup_inputs(seed, part) draws one part's arguments, and reference() takes and returns one part's arrays. A program takes and returns all parts, laid end to end along the dimension named above; an argument that names none is the same for every part. Nothing has to cross between parts.
All inputs are finite; a program needn't handle non-finite values.
Results may differ from the reference program's by a relative error of at most 0.014.
Values may be sent and summed in bfloat16 or wider, within the bound.
A program may use at most 128 MiB of HBM per device.

```python
import jax
import jax.numpy as jnp
from jax import lax

C = 256
HEADS = 8
BLOCKS = 2
ROWS = 16
COLS = 64
MEMBERS = 64
CELLS = 1024
N_MEM = 16


def draw_field(key, part):
    common_key = jax.random.fold_in(key, 11)
    member_key = jax.random.fold_in(key, 12)
    scale_key = jax.random.fold_in(key, 13)
    cell_key = jax.random.fold_in(key, 14)
    full_shape = (MEMBERS, ROWS, COLS, C)
    common = jax.random.normal(common_key, (1, ROWS, COLS, C), jnp.float32)
    perturb = jax.random.normal(member_key, full_shape, jnp.float32)
    cell_scale = jnp.exp(jax.random.uniform(cell_key, (1, ROWS, COLS, 1), jnp.float32, jnp.log(0.5), jnp.log(2.0)))
    member_scale = jnp.exp(jax.random.uniform(scale_key, (MEMBERS, 1, 1, 1), jnp.float32, jnp.log(0.3), jnp.log(1.5)))
    return jnp.clip((common + member_scale * perturb) * cell_scale, -8.0, 8.0).astype(jnp.bfloat16)


def draw_qkv_weight(key, part):
    weight_key = jax.random.fold_in(key, 21)
    baseline = jax.random.normal(weight_key, (BLOCKS, C, 3 * C), jnp.float32) * C ** (-0.5)
    return jnp.clip(baseline, -8.0, 8.0).astype(jnp.bfloat16)


def gaussian(rng, shape, spread, most, dtype=jnp.bfloat16):
    drawn = jax.random.normal(rng, shape, jnp.float32) * spread
    return jnp.minimum(jnp.maximum(drawn, -most), most).astype(dtype)


def setup_inputs(seed: int = 0, part: int = 0) -> dict:
    streams_of = jax.random.split(jax.random.key(seed), 6)
    part_keys = jax.random.split(jax.random.fold_in(streams_of[5], part), 6)
    return {
        "field": draw_field(jax.random.fold_in(jax.random.fold_in(streams_of[5], part), 71), part),
        "norm_gain": jnp.clip(1.0 + 0.18 * jax.random.normal(streams_of[1], (BLOCKS, 2, C), jnp.float32), 0.1, 1.9),
        "conv_weight": gaussian(streams_of[2], (BLOCKS, 3, 3, C, 2 * C), (9 * C) ** -0.5, 0.125),
        "qkv_weight": draw_qkv_weight(jax.random.fold_in(streams_of[5], 71), part),
        "out_weight": gaussian(streams_of[4], (BLOCKS, C, C), C ** -0.5, 0.375),
    }


epsilon = 1e-06

def rounded(values):
    return lax.optimization_barrier(values.astype(jnp.bfloat16))

def rms_norm(hidden_state, gain_row):
    widened = hidden_state.astype(jnp.float32)
    inverse = lax.rsqrt(lax.optimization_barrier(jnp.mean(widened * widened, axis=-1, keepdims=True)) + epsilon)
    return rounded(widened * inverse * gain_row)

def attend(cell_group, channels):
    head_size = channels // HEADS
    all_members, group_cells, _ = cell_group.shape
    widened = cell_group.astype(jnp.float32)
    queries = widened[:, :, :channels].reshape(all_members, group_cells, HEADS, head_size)
    keys_split = widened[:, :, channels:2 * channels].reshape(all_members, group_cells, HEADS, head_size)
    values_split = widened[:, :, 2 * channels:].reshape(all_members, group_cells, HEADS, head_size)
    scores = jnp.einsum('mchd,nchd->chmn', queries, keys_split, precision=lax.Precision.HIGHEST) * head_size ** (-0.5)
    row_max = lax.optimization_barrier(jnp.max(scores, axis=-1, keepdims=True))
    expo = jnp.exp(scores - row_max)
    probs = rounded(expo / lax.optimization_barrier(jnp.sum(expo, axis=-1, keepdims=True))).astype(jnp.float32)
    mixed = jnp.einsum('chmn,nchd->mchd', probs, values_split, precision=lax.Precision.HIGHEST)
    return rounded(mixed.reshape(all_members, group_cells, channels))

def reference(field, norm_gain, conv_weight, qkv_weight, out_weight):
    hidden_state = field
    channels = field.shape[-1]
    for layer_index in range(BLOCKS):
        normed = rms_norm(hidden_state, norm_gain[layer_index, 0])
        conv_out = lax.conv_general_dilated(normed.astype(jnp.float32), conv_weight[layer_index].astype(jnp.float32), (1, 1), 'SAME', dimension_numbers=('NHWC', 'HWIO', 'NHWC'), precision=lax.Precision.HIGHEST)
        value_part = conv_out[..., :channels]
        gate_part = conv_out[..., channels:]
        hidden_state = (hidden_state.astype(jnp.float32) + value_part * jax.nn.sigmoid(gate_part)).astype(jnp.bfloat16)
        normed2 = rms_norm(hidden_state, norm_gain[layer_index, 1]).reshape(MEMBERS * CELLS, channels)
        projected = rounded(jnp.dot(normed2, qkv_weight[layer_index], preferred_element_type=jnp.float32))
        grouped = projected.reshape(MEMBERS, N_MEM, CELLS // N_MEM, 3 * channels).transpose(1, 0, 2, 3)
        attended = lax.map(lambda cell_group: attend(cell_group, channels), grouped)
        attended = attended.transpose(1, 0, 2, 3).reshape(MEMBERS * CELLS, channels)
        update = jnp.dot(attended, out_weight[layer_index], preferred_element_type=jnp.float32)
        hidden_state = (hidden_state.astype(jnp.float32) + update.reshape(hidden_state.shape)).astype(jnp.bfloat16)
    return hidden_state
```

```python
import functools

import jax
import jax.numpy as jnp
from jax import lax
from jax.experimental import pallas as pl
from jax.experimental.pallas import tpu as pltpu
from jax.sharding import PartitionSpec as P

HEADS = 8
BLOCKS = 2
epsilon = 1e-06
VMEM_LIMIT = 58 * 1024 * 1024


def normalised(x, gain):
    inverse = lax.rsqrt(jnp.mean(x * x, axis=-1, keepdims=True) + epsilon)
    return x * inverse * gain


def gated(x, conv_out):
    channels = x.shape[-1]
    gate = conv_out[:, channels:]
    return x + conv_out[:, :channels] * (1.0 / (1.0 + jnp.exp(-gate)))


def taps(wide_ref, weight_ref, row, step):
    total = None
    for di in range(3):
        lhs = wide_ref[pl.ds(row + di, step)]
        lhs = lhs.reshape(-1, lhs.shape[-1])
        part = jnp.dot(lhs, weight_ref[di], preferred_element_type=jnp.float32)
        total = part if total is None else total + part
    return total


def conv_member_kernel(x_ref, gain_ref, weight_ref, out_ref, wide_ref):
    _, rows, cols, channels = x_ref.shape
    step = min(rows, 4)
    big = min(rows, 8)
    gain = gain_ref[...]
    zero = jnp.zeros((1, cols, 3 * channels), jnp.bfloat16)
    wide_ref[0:1] = zero
    wide_ref[rows + 1 : rows + 2] = zero
    flat = step * cols
    column = lax.broadcasted_iota(jnp.int32, (flat, channels), 0) % cols
    for row in range(0, rows, step):
        x = x_ref[0, row : row + step].astype(jnp.float32).reshape(flat, channels)
        normed = normalised(x, gain)
        left = jnp.where(column == 0, 0.0, pltpu.roll(normed, 1, 0))
        right = jnp.where(column == cols - 1, 0.0, pltpu.roll(normed, flat - 1, 0))
        for at, value in enumerate((left, normed, right)):
            wide_ref[row + 1 : row + 1 + step, :, at * channels : (at + 1) * channels] = value.astype(
                jnp.bfloat16
            ).reshape(step, cols, channels)
    for row in range(0, rows, big):
        conv_out = taps(wide_ref, weight_ref, row, big)
        x = x_ref[0, row : row + big].astype(jnp.float32).reshape(big * cols, channels)
        out_ref[0, row : row + big] = (
            gated(x, conv_out).astype(jnp.bfloat16).reshape(big, cols, channels)
        )


def conv_member(field, gain_row, weight):
    members, rows, cols, channels = field.shape
    weight = weight.reshape(3, 3 * channels, 2 * channels)
    return pl.pallas_call(
        conv_member_kernel,
        grid=(members,),
        in_specs=[
            pl.BlockSpec((1, rows, cols, channels), lambda i: (i, 0, 0, 0)),
            pl.BlockSpec((1, channels), lambda i: (0, 0)),
            pl.BlockSpec((3, 3 * channels, 2 * channels), lambda i: (0, 0, 0)),
        ],
        out_specs=pl.BlockSpec((1, rows, cols, channels), lambda i: (i, 0, 0, 0)),
        out_shape=jax.ShapeDtypeStruct(field.shape, jnp.bfloat16),
        scratch_shapes=[pltpu.VMEM((rows + 2, cols, 3 * channels), jnp.bfloat16)],
        compiler_params=pltpu.CompilerParams(vmem_limit_bytes=VMEM_LIMIT),
        name="conv_member",
    )(field, gain_row.reshape(1, channels), weight)


def conv_cell_kernel(x_ref, left_ref, right_ref, gain_ref, weight_ref, out_ref, wide_ref):
    rows, cols, members, channels = x_ref.shape
    gain = gain_ref[...]
    zero = jnp.zeros((1, cols, members, 3 * channels), jnp.bfloat16)
    wide_ref[0:1] = zero
    wide_ref[rows + 1 : rows + 2] = zero

    @pl.loop(0, rows)
    def _(row):
        def normed_of(ref, col):
            x = ref[row, col].astype(jnp.float32)
            return normalised(x, gain).astype(jnp.bfloat16)

        for col in range(-1, cols + 1):
            if col < 0:
                value = normed_of(left_ref, 0)
            elif col == cols:
                value = normed_of(right_ref, 0)
            else:
                value = normed_of(x_ref, col)
            for dj in range(3):
                target = col + 1 - dj
                if 0 <= target < cols:
                    wide_ref[row + 1, target, :, dj * channels : (dj + 1) * channels] = value

    step = max(1, min(rows, 512 // (cols * members)))

    @pl.loop(0, rows // step)
    def _(index):
        row = index * step
        conv_out = taps(wide_ref, weight_ref, row, step)
        x = x_ref[pl.ds(row, step)].astype(jnp.float32).reshape(-1, channels)
        out_ref[pl.ds(row, step)] = (
            gated(x, conv_out).astype(jnp.bfloat16).reshape(step, cols, members, channels)
        )


def conv_cell(state, left, right, gain_row, weight):
    rows, cols, members, channels = state.shape
    weight = weight.reshape(3, 3 * channels, 2 * channels)
    return pl.pallas_call(
        conv_cell_kernel,
        in_specs=[pl.BlockSpec(memory_space=pltpu.VMEM)] * 5,
        out_specs=pl.BlockSpec(memory_space=pltpu.VMEM),
        out_shape=jax.ShapeDtypeStruct(state.shape, jnp.bfloat16),
        scratch_shapes=[pltpu.VMEM((rows + 2, cols, members, 3 * channels), jnp.bfloat16)],
        compiler_params=pltpu.CompilerParams(vmem_limit_bytes=VMEM_LIMIT),
        name="conv_cell",
    )(state, left, right, gain_row.reshape(1, channels), weight)


def attend_block(x, gain, qkv_ref, out_w_ref, ones_ref):
    cells, members, channels = x.shape
    head_size = channels // HEADS
    scale = head_size ** (-0.5)
    rows = x.astype(jnp.float32).reshape(cells * members, channels)
    normed = normalised(rows, gain).astype(jnp.bfloat16)
    projected = jnp.dot(normed, qkv_ref[...], preferred_element_type=jnp.float32).astype(
        jnp.bfloat16
    )
    lane_head = lax.broadcasted_iota(jnp.int32, (members, channels), 1) // head_size
    masks = [lane_head == h for h in range(HEADS)]
    zero = jnp.zeros((members, channels), jnp.bfloat16)
    per = max(1, 128 // members)
    width = per * members
    lane_slot = lax.broadcasted_iota(jnp.int32, (members, width), 1) // members
    weights, mixed = [], []
    for cell in range(cells):
        block = projected[cell * members : (cell + 1) * members]
        queries = block[:, :channels]
        keys = block[:, channels : 2 * channels]
        values = block[:, 2 * channels :]
        spread_keys = jnp.concatenate([jnp.where(m, keys, zero) for m in masks], axis=0)
        spread_values = jnp.concatenate([jnp.where(m, values, zero) for m in masks], axis=0)
        scores = lax.dot_general(
            queries, spread_keys, (((1,), (1,)), ((), ())), preferred_element_type=jnp.float32
        )
        parts = []
        for tile in range(HEADS // per):
            s = scores[:, tile * width : (tile + 1) * width]
            if per == 1:
                most = jnp.max(s, axis=-1, keepdims=True)
            else:
                most = jnp.zeros_like(s)
                for slot in range(per):
                    here = lane_slot == slot
                    top = jnp.max(jnp.where(here, s, -jnp.inf), axis=-1, keepdims=True)
                    most = jnp.where(here, top, most)
            parts.append(jnp.exp((s - most) * scale).astype(jnp.bfloat16))
        weight = jnp.concatenate(parts, axis=1)
        weights.append(weight)
        mixed.append(jnp.dot(weight, spread_values, preferred_element_type=jnp.float32))
    weight = jnp.concatenate(weights, axis=0)
    total = jnp.dot(weight, ones_ref[...], preferred_element_type=jnp.float32)
    attended = (jnp.concatenate(mixed, axis=0) / total).astype(jnp.bfloat16)
    update = jnp.dot(attended, out_w_ref[...], preferred_element_type=jnp.float32)
    return (rows + update).astype(jnp.bfloat16).reshape(x.shape)


def attend_kernel(x_ref, gain_ref, qkv_ref, out_w_ref, ones_ref, out_ref):
    out_ref[...] = attend_block(x_ref[...], gain_ref[...], qkv_ref, out_w_ref, ones_ref)


def head_sums(members, channels):
    row = jnp.arange(HEADS * members)[:, None] // members
    lane = jnp.arange(channels)[None, :] // (channels // HEADS)
    return (row == lane).astype(jnp.bfloat16)


def attend(state, gain_row, qkv, out_w):
    cells, members, channels = state.shape
    block = max(1, min(cells, 512 // members))
    spec = pl.BlockSpec((block, members, channels), lambda i: (i, 0, 0))
    return pl.pallas_call(
        attend_kernel,
        grid=(cells // block,),
        in_specs=[
            spec,
            pl.BlockSpec((1, channels), lambda i: (0, 0)),
            pl.BlockSpec((channels, 3 * channels), lambda i: (0, 0)),
            pl.BlockSpec((channels, channels), lambda i: (0, 0)),
            pl.BlockSpec((HEADS * members, channels), lambda i: (0, 0)),
        ],
        out_specs=spec,
        out_shape=jax.ShapeDtypeStruct(state.shape, jnp.bfloat16),
        compiler_params=pltpu.CompilerParams(vmem_limit_bytes=VMEM_LIMIT),
        name="attend",
    )(state, gain_row.reshape(1, channels), qkv, out_w, head_sums(members, channels))


def body(field, norm_gain, conv_weight, qkv_weight, out_weight):
    members, rows, cols, channels = field.shape
    devices = lax.axis_size("mem")
    width = cols // devices
    all_members = members * devices
    forward = [(i, i + 1) for i in range(devices - 1)]
    backward = [(b, a) for a, b in forward]

    mine = conv_member(field, norm_gain[0, 0], conv_weight[0])
    split = mine.reshape(members, rows, devices, width, channels).transpose(2, 0, 1, 3, 4)
    arrived = lax.all_to_all(split, "mem", split_axis=0, concat_axis=0, tiled=True)
    state = arrived.reshape(all_members, rows * width, channels).transpose(1, 0, 2)
    state = attend(state, norm_gain[0, 1], qkv_weight[0], out_weight[0])
    for b in range(1, BLOCKS):
        grid = state.reshape(rows, width, all_members, channels)
        left = lax.ppermute(grid[:, -1:], "mem", forward)
        right = lax.ppermute(grid[:, :1], "mem", backward)
        grid = conv_cell(grid, left, right, norm_gain[b, 0], conv_weight[b])
        state = grid.reshape(rows * width, all_members, channels)
        state = attend(state, norm_gain[b, 1], qkv_weight[b], out_weight[b])
    back = state.transpose(1, 0, 2).reshape(devices, members, rows, width, channels)
    returned = lax.all_to_all(back, "mem", split_axis=0, concat_axis=0, tiled=True)
    return returned.transpose(1, 2, 0, 3, 4).reshape(members, rows, cols, channels)


def solution(mesh):
    return jax.shard_map(
        body,
        mesh=mesh,
        in_specs=(P(("grp", "mem"), None, None, None), P(), P(), P(), P()),
        out_specs=P(("grp", "mem"), None, None, None),
        check_vma=False,
    )
```

```python
import functools

import jax
import jax.numpy as jnp
from jax import lax
from jax.experimental import pallas as pl
from jax.experimental.pallas import tpu as pltpu
from jax.sharding import PartitionSpec as P

HEADS = 8
epsilon = 1e-06
VMEM_LIMIT = 58 * 1024 * 1024


def normalised(x, gain):
    inverse = lax.rsqrt(jnp.mean(x * x, axis=-1, keepdims=True) + epsilon)
    return x * inverse * gain


def gated(x, conv_out):
    channels = x.shape[-1]
    gate = conv_out[:, channels:]
    return x + conv_out[:, :channels] * (1.0 / (1.0 + jnp.exp(-gate)))


def taps(wide_ref, weight_ref, row, step):
    total = None
    for di in range(3):
        lhs = wide_ref[pl.ds(row + di, step)]
        lhs = lhs.reshape(-1, lhs.shape[-1])
        part = jnp.dot(lhs, weight_ref[di], preferred_element_type=jnp.float32)
        total = part if total is None else total + part
    return total


def conv_cell_kernel(x_ref, left_ref, right_ref, gain_ref, weight_ref, out_ref, wide_ref):
    rows, cols, members, channels = x_ref.shape
    gain = gain_ref[...]
    zero = jnp.zeros((1, cols, members, 3 * channels), jnp.bfloat16)
    wide_ref[0:1] = zero
    wide_ref[rows + 1 : rows + 2] = zero

    @pl.loop(0, rows)
    def _(row):
        def normed_of(ref, col):
            x = ref[row, col].astype(jnp.float32)
            return normalised(x, gain).astype(jnp.bfloat16)

        for col in range(-1, cols + 1):
            if col < 0:
                value = normed_of(left_ref, 0)
            elif col == cols:
                value = normed_of(right_ref, 0)
            else:
                value = normed_of(x_ref, col)
            for dj in range(3):
                target = col + 1 - dj
                if 0 <= target < cols:
                    wide_ref[row + 1, target, :, dj * channels : (dj + 1) * channels] = value

    step = max(1, min(rows, 512 // (cols * members)))

    @pl.loop(0, rows // step)
    def _(index):
        row = index * step
        conv_out = taps(wide_ref, weight_ref, row, step)
        x = x_ref[pl.ds(row, step)].astype(jnp.float32).reshape(-1, channels)
        out_ref[pl.ds(row, step)] = (
            gated(x, conv_out).astype(jnp.bfloat16).reshape(step, cols, members, channels)
        )


def conv_cell(state, left, right, gain_row, weight):
    rows, cols, members, channels = state.shape
    weight = weight.reshape(3, 3 * channels, 2 * channels)
    return pl.pallas_call(
        conv_cell_kernel,
        in_specs=[pl.BlockSpec(memory_space=pltpu.VMEM)] * 5,
        out_specs=pl.BlockSpec(memory_space=pltpu.VMEM),
        out_shape=jax.ShapeDtypeStruct(state.shape, jnp.bfloat16),
        scratch_shapes=[pltpu.VMEM((rows + 2, cols, members, 3 * channels), jnp.bfloat16)],
        compiler_params=pltpu.CompilerParams(vmem_limit_bytes=VMEM_LIMIT),
        name="conv_cell",
    )(state, left, right, gain_row.reshape(1, channels), weight)


def attend_block(x, gain, qkv_ref, out_w_ref, ones_ref):
    cells, members, channels = x.shape
    head_size = channels // HEADS
    scale = head_size ** (-0.5)
    rows = x.reshape(cells * members, channels)
    normed = normalised(rows, gain).astype(jnp.bfloat16)
    projected = jnp.dot(normed, qkv_ref[...], preferred_element_type=jnp.float32).astype(
        jnp.bfloat16
    )
    lane_head = lax.broadcasted_iota(jnp.int32, (members, channels), 1) // head_size
    masks = [lane_head == h for h in range(HEADS)]
    zero = jnp.zeros((members, channels), jnp.bfloat16)
    per = max(1, 128 // members)
    width = per * members
    lane_slot = lax.broadcasted_iota(jnp.int32, (members, width), 1) // members
    weights, mixed = [], []
    for cell in range(cells):
        block = projected[cell * members : (cell + 1) * members]
        queries = block[:, :channels]
        keys = block[:, channels : 2 * channels]
        values = block[:, 2 * channels :]
        spread_keys = jnp.concatenate([jnp.where(m, keys, zero) for m in masks], axis=0)
        spread_values = jnp.concatenate([jnp.where(m, values, zero) for m in masks], axis=0)
        scores = lax.dot_general(
            queries, spread_keys, (((1,), (1,)), ((), ())), preferred_element_type=jnp.float32
        )
        parts = []
        for tile in range(HEADS // per):
            s = scores[:, tile * width : (tile + 1) * width]
            if per == 1:
                most = jnp.max(s, axis=-1, keepdims=True)
            else:
                most = jnp.zeros_like(s)
                for slot in range(per):
                    here = lane_slot == slot
                    top = jnp.max(jnp.where(here, s, -jnp.inf), axis=-1, keepdims=True)
                    most = jnp.where(here, top, most)
            parts.append(jnp.exp((s - most) * scale).astype(jnp.bfloat16))
        weight = jnp.concatenate(parts, axis=1)
        weights.append(weight)
        mixed.append(jnp.dot(weight, spread_values, preferred_element_type=jnp.float32))
    weight = jnp.concatenate(weights, axis=0)
    total = jnp.dot(weight, ones_ref[...], preferred_element_type=jnp.float32)
    attended = (jnp.concatenate(mixed, axis=0) / total).astype(jnp.bfloat16)
    update = jnp.dot(attended, out_w_ref[...], preferred_element_type=jnp.float32)
    return (rows + update).reshape(x.shape)


def head_sums(members, channels):
    row = jnp.arange(HEADS * members)[:, None] // members
    lane = jnp.arange(channels)[None, :] // (channels // HEADS)
    return (row == lane).astype(jnp.bfloat16)


def enter(devices, me):
    barrier = pltpu.get_barrier_semaphore()

    @pl.loop(1, devices)
    def _(k):
        pl.semaphore_signal(
            barrier,
            inc=1,
            device_id={"mem": lax.rem(me + k, devices)},
            device_id_type=pl.DeviceIdType.MESH,
        )

    pl.semaphore_wait(barrier, devices - 1)


def exchange(source_of, target, me, devices, send_sem, recv_sem):
    own = pltpu.make_async_copy(source_of(me), target, recv_sem.at[me])
    own.start()

    @pl.loop(1, devices)
    def _(k):
        to = lax.rem(me + k, devices)
        pltpu.make_async_remote_copy(
            src_ref=source_of(to),
            dst_ref=target,
            send_sem=send_sem.at[to],
            recv_sem=recv_sem.at[me],
            device_id={"mem": to},
            device_id_type=pl.DeviceIdType.MESH,
        ).start()


def wait_all(ref, me, devices, sem, own):
    @pl.loop(0 if own else 1, devices)
    def _(k):
        pltpu.make_async_copy(ref, ref, sem.at[lax.rem(me + k, devices)]).wait()


def swap_strips(parts, width):
    count = len(parts)
    slot = lax.broadcasted_iota(jnp.int32, parts[0].shape, parts[0].ndim - 2) // width
    results = []
    for j in range(count):
        total = None
        for i in range(count):
            shift = ((i - j) * width) % (count * width)
            part = parts[i] if shift == 0 else pltpu.roll(parts[i], shift, parts[i].ndim - 2)
            total = part if total is None else jnp.where(slot == i, part, total)
        results.append(total)
    return results


def first_kernel(
    devices,
    x_ref,
    gain_ref,
    conv_ref,
    gain2_ref,
    qkv_ref,
    out_w_ref,
    ones_ref,
    out_ref,
    wide_ref,
    send_ref,
    recv_ref,
    send_sem,
    recv_sem,
):
    members, rows, cols, channels = x_ref.shape
    width = cols // devices
    batch = 8 // width
    chunks = rows // batch
    groups = cols // 8
    me = lax.axis_index("mem")
    gain = gain_ref[...]
    flat = batch * cols
    column = lax.broadcasted_iota(jnp.int32, (flat, channels), 0) % cols

    def fill(row):
        for member in range(members):
            x = x_ref[member, pl.ds(row, batch)].astype(jnp.float32).reshape(flat, channels)
            normed = normalised(x, gain)
            left = jnp.where(column == 0, 0.0, pltpu.roll(normed, 1, 0))
            right = jnp.where(column == cols - 1, 0.0, pltpu.roll(normed, flat - 1, 0))
            for at, value in enumerate((left, normed, right)):
                wide_ref[
                    member, pl.ds(row + 1, batch), :, at * channels : (at + 1) * channels
                ] = value.astype(jnp.bfloat16).reshape(batch, cols, channels)

    zero = jnp.zeros((members, 1, cols, 3 * channels), jnp.bfloat16)
    wide_ref[:, 0:1] = zero
    wide_ref[:, rows + 1 : rows + 2] = zero
    fill(0)
    enter(devices, me)

    @pl.loop(0, chunks)
    def _(q):
        row = q * batch

        @pl.when(q < chunks - 1)
        def _():
            fill(row + batch)

        total = None
        for di in range(3):
            lhs = wide_ref[:, pl.ds(row + di, batch)].reshape(members * flat, 3 * channels)
            part = jnp.dot(lhs, conv_ref[di], preferred_element_type=jnp.float32)
            total = part if total is None else total + part
        x = x_ref[:, pl.ds(row, batch)].astype(jnp.float32).reshape(members * flat, channels)
        y = gated(x, total).reshape(members, batch, groups, 8, channels)
        parts = swap_strips(
            [y[:, i].reshape(members * groups, 8, channels) for i in range(batch)], width
        )
        for j in range(batch):
            part = parts[j].astype(jnp.bfloat16).reshape(members, groups, 8, channels)
            for k in range(groups):
                send_ref[q, k * batch + j] = part[:, k]
        exchange(
            lambda d: send_ref.at[q, d],
            recv_ref.at[q, me],
            me,
            devices,
            send_sem.at[q],
            recv_sem.at[q],
        )

    @pl.loop(0, chunks)
    def _(q):
        wait_all(recv_ref.at[q, 0], me, devices, recv_sem.at[q], True)
        x = recv_ref[q].astype(jnp.float32).reshape(devices * members, 8, channels)
        x = jnp.transpose(x, (1, 0, 2))
        y = attend_block(x, gain2_ref[...], qkv_ref, out_w_ref, ones_ref)
        out_ref[pl.ds(q * 8, 8)] = y.astype(jnp.bfloat16)

    @pl.loop(0, chunks)
    def _(q):
        wait_all(send_ref.at[q, 0], me, devices, send_sem.at[q], False)


def last_kernel(
    devices,
    x_ref,
    gain2_ref,
    qkv_ref,
    out_w_ref,
    ones_ref,
    out_ref,
    send_ref,
    recv_ref,
    send_sem,
    recv_sem,
):
    members, rows, cols, channels = out_ref.shape
    width = cols // devices
    batch = 8 // width
    chunks = rows // batch
    groups = cols // 8
    me = lax.axis_index("mem")
    enter(devices, me)

    @pl.loop(0, chunks)
    def _(q):
        x = x_ref[pl.ds(q * 8, 8)].astype(jnp.float32)
        y = attend_block(x, gain2_ref[...], qkv_ref, out_w_ref, ones_ref)
        y = jnp.transpose(y, (1, 0, 2)).astype(jnp.bfloat16)
        send_ref[q] = y.reshape(devices, members, 8, channels)
        exchange(
            lambda d: send_ref.at[q, d],
            recv_ref.at[q, me],
            me,
            devices,
            send_sem.at[q],
            recv_sem.at[q],
        )

    @pl.loop(0, chunks)
    def _(q):
        wait_all(recv_ref.at[q, 0], me, devices, recv_sem.at[q], True)
        parts = []
        for j in range(batch):
            part = [recv_ref[q, k * batch + j].astype(jnp.float32) for k in range(groups)]
            parts.append(jnp.concatenate(part, axis=0))
        for i, part in enumerate(swap_strips(parts, width)):
            part = part.reshape(groups, members, 8, channels)
            for member in range(members):
                line = jnp.concatenate([part[k, member] for k in range(groups)], axis=0)
                out_ref[member, q * batch + i] = line.astype(jnp.bfloat16)

    @pl.loop(0, chunks)
    def _(q):
        wait_all(send_ref.at[q, 0], me, devices, send_sem.at[q], False)


def whole(count):
    return [pl.BlockSpec(memory_space=pltpu.VMEM)] * count


def transfers(chunks, devices, members, channels):
    block = pltpu.VMEM((chunks, devices, members, 8, channels), jnp.bfloat16)
    sems = pltpu.SemaphoreType.DMA((chunks, devices))
    return [block, block, sems, sems]


def first(field, gain, weight, gain2, qkv, out_w, devices):
    members, rows, cols, channels = field.shape
    batch = 8 // (cols // devices)
    cells = rows * cols // devices
    shape = (cells, members * devices, channels)
    return pl.pallas_call(
        functools.partial(first_kernel, devices),
        in_specs=whole(7),
        out_specs=pl.BlockSpec(memory_space=pltpu.VMEM),
        out_shape=jax.ShapeDtypeStruct(shape, jnp.bfloat16),
        scratch_shapes=[
            pltpu.VMEM((members, rows + 2, cols, 3 * channels), jnp.bfloat16),
            *transfers(rows // batch, devices, members, channels),
        ],
        compiler_params=pltpu.CompilerParams(
            vmem_limit_bytes=VMEM_LIMIT, collective_id=0, has_side_effects=True
        ),
        name="conv_scatter_attend",
    )(
        field,
        gain.reshape(1, channels),
        weight.reshape(3, 3 * channels, 2 * channels),
        gain2.reshape(1, channels),
        qkv,
        out_w,
        head_sums(members * devices, channels),
    )


def last(state, gain2, qkv, out_w, shape, devices):
    members, rows, cols, channels = shape
    batch = 8 // (cols // devices)
    return pl.pallas_call(
        functools.partial(last_kernel, devices),
        in_specs=whole(5),
        out_specs=pl.BlockSpec(memory_space=pltpu.VMEM),
        out_shape=jax.ShapeDtypeStruct(shape, jnp.bfloat16),
        scratch_shapes=transfers(rows // batch, devices, members, channels),
        compiler_params=pltpu.CompilerParams(
            vmem_limit_bytes=VMEM_LIMIT, collective_id=1, has_side_effects=True
        ),
        name="attend_gather",
    )(
        state,
        gain2.reshape(1, channels),
        qkv,
        out_w,
        head_sums(members * devices, channels),
    )


def body(field, norm_gain, conv_weight, qkv_weight, out_weight):
    members, rows, cols, channels = field.shape
    devices = lax.axis_size("mem")
    width = cols // devices
    forward = [(i, i + 1) for i in range(devices - 1)]
    backward = [(b, a) for a, b in forward]
    state = first(
        field, norm_gain[0, 0], conv_weight[0], norm_gain[0, 1], qkv_weight[0], out_weight[0], devices
    )
    grid = state.reshape(rows, width, members * devices, channels)
    left = lax.ppermute(grid[:, -1:], "mem", forward)
    right = lax.ppermute(grid[:, :1], "mem", backward)
    grid = conv_cell(grid, left, right, norm_gain[1, 0], conv_weight[1])
    state = grid.reshape(state.shape)
    return last(state, norm_gain[1, 1], qkv_weight[1], out_weight[1], field.shape, devices)


def solution(mesh):
    return jax.shard_map(
        body,
        mesh=mesh,
        in_specs=(P(("grp", "mem"), None, None, None), P(), P(), P(), P()),
        out_specs=P(("grp", "mem"), None, None, None),
        check_vma=False,
    )
```

```python
import functools

import jax
import jax.numpy as jnp
from jax import lax
from jax.experimental import pallas as pl
from jax.experimental.pallas import tpu as pltpu
from jax.sharding import PartitionSpec as P

HEADS = 8
epsilon = 1e-06
VMEM_LIMIT = 58 * 1024 * 1024


def normalised(x, gain):
    inverse = lax.rsqrt(jnp.mean(x * x, axis=-1, keepdims=True) + epsilon)
    return x * inverse * gain


def gated(x, conv_out):
    channels = x.shape[-1]
    gate = conv_out[:, channels:]
    return x + conv_out[:, :channels] * (1.0 / (1.0 + jnp.exp(-gate)))


def taps(rows_of, weight_ref):
    total = None
    for di in range(3):
        lhs = rows_of(di)
        lhs = lhs.reshape(-1, lhs.shape[-1])
        weight = weight_ref[di].reshape(lhs.shape[-1], -1)
        part = jnp.dot(lhs, weight, preferred_element_type=jnp.float32)
        total = part if total is None else total + part
    return total


def attend_block(x, gain, qkv, out_w, ones_ref):
    cells, members, channels = x.shape
    head_size = channels // HEADS
    scale = head_size ** (-0.5)
    rows = x.reshape(cells * members, channels)
    normed = normalised(rows, gain).astype(jnp.bfloat16)
    projected = jnp.dot(normed, qkv, preferred_element_type=jnp.float32).astype(
        jnp.bfloat16
    )
    lane_head = lax.broadcasted_iota(jnp.int32, (members, channels), 1) // head_size
    masks = [lane_head == h for h in range(HEADS)]
    zero = jnp.zeros((members, channels), jnp.bfloat16)
    per = max(1, 128 // members)
    width = per * members
    lane_slot = lax.broadcasted_iota(jnp.int32, (members, width), 1) // members
    weights, mixed = [], []
    for cell in range(cells):
        block = projected[cell * members : (cell + 1) * members]
        queries = block[:, :channels]
        keys = block[:, channels : 2 * channels]
        values = block[:, 2 * channels :]
        spread_keys = jnp.concatenate([jnp.where(m, keys, zero) for m in masks], axis=0)
        spread_values = jnp.concatenate([jnp.where(m, values, zero) for m in masks], axis=0)
        scores = lax.dot_general(
            queries, spread_keys, (((1,), (1,)), ((), ())), preferred_element_type=jnp.float32
        )
        parts = []
        for tile in range(HEADS // per):
            s = scores[:, tile * width : (tile + 1) * width]
            if per == 1:
                most = jnp.max(s, axis=-1, keepdims=True)
            else:
                most = jnp.zeros_like(s)
                for slot in range(per):
                    here = lane_slot == slot
                    top = jnp.max(jnp.where(here, s, -jnp.inf), axis=-1, keepdims=True)
                    most = jnp.where(here, top, most)
            parts.append(jnp.exp((s - most) * scale).astype(jnp.bfloat16))
        weight = jnp.concatenate(parts, axis=1)
        weights.append(weight)
        mixed.append(jnp.dot(weight, spread_values, preferred_element_type=jnp.float32))
    weight = jnp.concatenate(weights, axis=0)
    total = jnp.dot(weight, ones_ref[...], preferred_element_type=jnp.float32)
    attended = (jnp.concatenate(mixed, axis=0) / total).astype(jnp.bfloat16)
    update = jnp.dot(attended, out_w, preferred_element_type=jnp.float32)
    return (rows + update).reshape(x.shape)


def enter(devices, me):
    barrier = pltpu.get_barrier_semaphore()

    @pl.loop(1, devices)
    def _(k):
        pl.semaphore_signal(
            barrier,
            inc=1,
            device_id={"mem": lax.rem(me + k, devices)},
            device_id_type=pl.DeviceIdType.MESH,
        )

    pl.semaphore_wait(barrier, devices - 1)


def exchange(source_of, target, me, devices, send_sem, recv_sem):
    own = pltpu.make_async_copy(source_of(me), target, recv_sem.at[me])
    own.start()

    @pl.loop(1, devices)
    def _(k):
        to = lax.rem(me + k, devices)
        pltpu.make_async_remote_copy(
            src_ref=source_of(to),
            dst_ref=target,
            send_sem=send_sem.at[to],
            recv_sem=recv_sem.at[me],
            device_id={"mem": to},
            device_id_type=pl.DeviceIdType.MESH,
        ).start()


def wait_all(ref, me, devices, sem, own):
    @pl.loop(0 if own else 1, devices)
    def _(k):
        pltpu.make_async_copy(ref, ref, sem.at[lax.rem(me + k, devices)]).wait()


def swap_strips(parts, width):
    count = len(parts)
    slot = lax.broadcasted_iota(jnp.int32, parts[0].shape, parts[0].ndim - 2) // width
    results = []
    for j in range(count):
        total = None
        for i in range(count):
            shift = ((i - j) * width) % (count * width)
            part = parts[i] if shift == 0 else pltpu.roll(parts[i], shift, parts[i].ndim - 2)
            total = part if total is None else jnp.where(slot == i, part, total)
        results.append(total)
    return results


def kernel(
    devices,
    x_ref,
    gain_ref,
    conv_hbm,
    qkv_ref,
    out_w_ref,
    out_ref,
    conv_ref,
    ones_ref,
    wide_ref,
    wide2_ref,
    state_ref,
    left_ref,
    right_ref,
    send_ref,
    recv_ref,
    send2_ref,
    recv2_ref,
    conv_sem,
    send_sem,
    recv_sem,
    send2_sem,
    recv2_sem,
    edge_send,
    edge_recv,
):
    members, rows, cols, channels = x_ref.shape
    width = cols // devices
    batch = 8 // width
    chunks = rows // batch
    groups = cols // 8
    everyone = members * devices
    me = lax.axis_index("mem")
    flat = batch * cols
    column = lax.broadcasted_iota(jnp.int32, (flat, channels), 0) % cols
    loads = [
        pltpu.make_async_copy(conv_hbm.at[b], conv_ref.at[b], conv_sem.at[b]) for b in range(2)
    ]
    for load in loads:
        load.start()

    def fill(row):
        for member in range(members):
            x = x_ref[member, pl.ds(row, batch)].astype(jnp.float32).reshape(flat, channels)
            normed = normalised(x, gain_ref[0, 0:1])
            left = jnp.where(column == 0, 0.0, pltpu.roll(normed, 1, 0))
            right = jnp.where(column == cols - 1, 0.0, pltpu.roll(normed, flat - 1, 0))
            for at, value in enumerate((left, normed, right)):
                wide_ref[
                    member, pl.ds(row + 1, batch), :, at * channels : (at + 1) * channels
                ] = value.astype(jnp.bfloat16).reshape(batch, cols, channels)

    zero = jnp.zeros((members, 1, cols, 3 * channels), jnp.bfloat16)
    wide_ref[:, 0:1] = zero
    wide_ref[:, rows + 1 : rows + 2] = zero
    fill(0)
    enter(devices, me)
    loads[0].wait()

    @pl.loop(0, chunks)
    def _(q):
        row = q * batch

        @pl.when(q < chunks - 1)
        def _():
            fill(row + batch)

        total = taps(lambda di: wide_ref[:, pl.ds(row + di, batch)], conv_ref.at[0])
        x = x_ref[:, pl.ds(row, batch)].astype(jnp.float32).reshape(members * flat, channels)
        y = gated(x, total).reshape(members, batch, groups, 8, channels)
        parts = swap_strips(
            [y[:, i].reshape(members * groups, 8, channels) for i in range(batch)], width
        )
        for j in range(batch):
            part = parts[j].astype(jnp.bfloat16).reshape(members, groups, 8, channels)
            for k in range(groups):
                send_ref[q, k * batch + j] = part[:, k]
        exchange(
            lambda d: send_ref.at[q, d],
            recv_ref.at[q, me],
            me,
            devices,
            send_sem.at[q],
            recv_sem.at[q],
        )

    head_of_row = lax.broadcasted_iota(jnp.int32, ones_ref.shape, 0) // everyone
    head_of_lane = lax.broadcasted_iota(jnp.int32, ones_ref.shape, 1) // (channels // HEADS)
    ones_ref[...] = jnp.where(head_of_row == head_of_lane, 1.0, 0.0).astype(jnp.bfloat16)
    edge = jnp.zeros((1, width, everyone, 3 * channels), jnp.bfloat16)
    wide2_ref[0:1] = edge
    wide2_ref[rows + 1 : rows + 2] = edge

    @pl.when(me == 0)
    def _():
        left_ref[...] = jnp.zeros_like(left_ref)

    @pl.when(me == devices - 1)
    def _():
        right_ref[...] = jnp.zeros_like(right_ref)

    def to_right(q):
        span = pl.ds(q * batch, batch)
        return pltpu.make_async_remote_copy(
            src_ref=state_ref.at[span, width - 1],
            dst_ref=left_ref.at[span],
            send_sem=edge_send.at[0, q],
            recv_sem=edge_recv.at[0, q],
            device_id={"mem": lax.rem(me + 1, devices)},
            device_id_type=pl.DeviceIdType.MESH,
        )

    def to_left(q):
        span = pl.ds(q * batch, batch)
        return pltpu.make_async_remote_copy(
            src_ref=state_ref.at[span, 0],
            dst_ref=right_ref.at[span],
            send_sem=edge_send.at[1, q],
            recv_sem=edge_recv.at[1, q],
            device_id={"mem": lax.rem(me + devices - 1, devices)},
            device_id_type=pl.DeviceIdType.MESH,
        )

    def fill2(q):
        @pl.when(me > 0)
        def _():
            to_right(q).wait_recv()

        @pl.when(me < devices - 1)
        def _():
            to_left(q).wait_recv()

        for step in range(batch):
            row = q * batch + step
            for col in range(-1, width + 1):
                if col < 0:
                    x = left_ref[row]
                elif col == width:
                    x = right_ref[row]
                else:
                    x = state_ref[row, col]
                value = normalised(x.astype(jnp.float32), gain_ref[1, 0:1]).astype(jnp.bfloat16)
                for dj in range(3):
                    target = col + 1 - dj
                    if 0 <= target < width:
                        wide2_ref[row + 1, target, :, dj * channels : (dj + 1) * channels] = value

    @pl.loop(0, chunks + 2)
    def _(q):
        @pl.when(q < chunks)
        def _():
            wait_all(recv_ref.at[q, 0], me, devices, recv_sem.at[q], True)
            x = recv_ref[q].astype(jnp.float32).reshape(everyone, 8, channels)
            x = jnp.transpose(x, (1, 0, 2))
            y = attend_block(x, gain_ref[0, 1:2], qkv_ref[0], out_w_ref[0], ones_ref)
            y = y.astype(jnp.bfloat16).reshape(batch, width, everyone, channels)
            state_ref[pl.ds(q * batch, batch)] = y

            @pl.when(me < devices - 1)
            def _():
                to_right(q).start()

            @pl.when(me > 0)
            def _():
                to_left(q).start()

        @pl.when(q == 1)
        def _():
            loads[1].wait()

        @pl.when((q >= 1) & (q <= chunks))
        def _():
            fill2(q - 1)

        @pl.when(q >= 2)
        def _():
            p = q - 2
            row = p * batch
            total = taps(lambda di: wide2_ref[pl.ds(row + di, batch)], conv_ref.at[1])
            x = state_ref[pl.ds(row, batch)].astype(jnp.float32).reshape(-1, channels)
            x = gated(x, total).astype(jnp.bfloat16).astype(jnp.float32)
            x = x.reshape(8, everyone, channels)
            y = attend_block(x, gain_ref[1, 1:2], qkv_ref[1], out_w_ref[1], ones_ref)
            y = jnp.transpose(y, (1, 0, 2)).astype(jnp.bfloat16)
            send2_ref[p] = y.reshape(devices, members, 8, channels)
            exchange(
                lambda d: send2_ref.at[p, d],
                recv2_ref.at[p, me],
                me,
                devices,
                send2_sem.at[p],
                recv2_sem.at[p],
            )

    @pl.loop(0, chunks)
    def _(q):
        wait_all(send_ref.at[q, 0], me, devices, send_sem.at[q], False)

        @pl.when(me < devices - 1)
        def _():
            to_right(q).wait_send()

        @pl.when(me > 0)
        def _():
            to_left(q).wait_send()

    @pl.loop(0, chunks)
    def _(q):
        wait_all(recv2_ref.at[q, 0], me, devices, recv2_sem.at[q], True)
        parts = []
        for j in range(batch):
            part = [recv2_ref[q, k * batch + j].astype(jnp.float32) for k in range(groups)]
            parts.append(jnp.concatenate(part, axis=0))
        for i, part in enumerate(swap_strips(parts, width)):
            part = part.reshape(groups, members, 8, channels)
            for member in range(members):
                line = jnp.concatenate([part[k, member] for k in range(groups)], axis=0)
                out_ref[member, q * batch + i] = line.astype(jnp.bfloat16)

    @pl.loop(0, chunks)
    def _(q):
        wait_all(send2_ref.at[q, 0], me, devices, send2_sem.at[q], False)


def body(field, norm_gain, conv_weight, qkv_weight, out_weight):
    members, rows, cols, channels = field.shape
    devices = lax.axis_size("mem")
    width = cols // devices
    chunks = rows * width // 8
    everyone = members * devices
    vmem = lambda *shape: pltpu.VMEM(shape, jnp.bfloat16)
    block = vmem(chunks, devices, members, 8, channels)
    sems = pltpu.SemaphoreType.DMA((chunks, devices))
    edges = pltpu.SemaphoreType.DMA((2, chunks))
    here = pl.BlockSpec(memory_space=pltpu.VMEM)
    return pl.pallas_call(
        functools.partial(kernel, devices),
        in_specs=[here, here, pl.BlockSpec(memory_space=pl.ANY), here, here],
        out_specs=here,
        out_shape=jax.ShapeDtypeStruct(field.shape, jnp.bfloat16),
        scratch_shapes=[
            vmem(*conv_weight.shape),
            vmem(HEADS * everyone, channels),
            vmem(members, rows + 2, cols, 3 * channels),
            vmem(rows + 2, width, everyone, 3 * channels),
            vmem(rows, width, everyone, channels),
            vmem(rows, everyone, channels),
            vmem(rows, everyone, channels),
            block,
            block,
            block,
            block,
            pltpu.SemaphoreType.DMA((2,)),
            sems,
            sems,
            sems,
            sems,
            edges,
            edges,
        ],
        compiler_params=pltpu.CompilerParams(
            vmem_limit_bytes=VMEM_LIMIT, collective_id=0, has_side_effects=True
        ),
        name="transformer",
    )(field, norm_gain, conv_weight, qkv_weight, out_weight)


def solution(mesh):
    return jax.shard_map(
        body,
        mesh=mesh,
        in_specs=(P(("grp", "mem"), None, None, None), P(), P(), P(), P()),
        out_specs=P(("grp", "mem"), None, None, None),
        check_vma=False,
    )
```

```python
import functools
import math

import jax
import jax.numpy as jnp
from jax import lax
from jax.experimental import pallas as pl
from jax.experimental.pallas import tpu as pltpu
from jax.sharding import PartitionSpec as P

HEADS = 8
epsilon = 1e-06
OUTWARD = 2
HOMEWARD = 2
VMEM_LIMIT = 58 * 1024 * 1024


def normalised(x, gain):
    inverse = lax.rsqrt(jnp.mean(x * x, axis=-1, keepdims=True) + epsilon)
    return x * inverse * gain


def gated(x, conv_out):
    channels = x.shape[-1]
    gate = conv_out[:, channels:]
    return x + conv_out[:, :channels] * (1.0 / (1.0 + jnp.exp(-gate)))


def taps(rows_of, weight_ref):
    total = None
    for di in range(3):
        lhs = rows_of(di)
        lhs = lhs.reshape(-1, lhs.shape[-1])
        weight = weight_ref[di].reshape(lhs.shape[-1], -1)
        part = jnp.dot(lhs, weight, preferred_element_type=jnp.float32)
        total = part if total is None else total + part
    return total


def attend_block(x, gain, qkv, out_w, ones_ref):
    cells, members, channels = x.shape
    head_size = channels // HEADS
    scale = head_size ** (-0.5)
    rows = x.reshape(cells * members, channels)
    normed = normalised(rows, gain).astype(jnp.bfloat16)
    projected = jnp.dot(normed, qkv, preferred_element_type=jnp.float32).astype(
        jnp.bfloat16
    )
    lane_head = lax.broadcasted_iota(jnp.int32, (members, channels), 1) // head_size
    masks = [lane_head == h for h in range(HEADS)]
    zero = jnp.zeros((members, channels), jnp.bfloat16)
    per = max(1, 128 // members)
    width = per * members
    lane_slot = lax.broadcasted_iota(jnp.int32, (members, width), 1) // members
    weights, mixed = [], []
    for cell in range(cells):
        block = projected[cell * members : (cell + 1) * members]
        queries = block[:, :channels]
        keys = block[:, channels : 2 * channels]
        values = block[:, 2 * channels :]
        spread_keys = jnp.concatenate([jnp.where(m, keys, zero) for m in masks], axis=0)
        spread_values = jnp.concatenate([jnp.where(m, values, zero) for m in masks], axis=0)
        scores = lax.dot_general(
            queries, spread_keys, (((1,), (1,)), ((), ())), preferred_element_type=jnp.float32
        )
        parts = []
        for tile in range(HEADS // per):
            s = scores[:, tile * width : (tile + 1) * width]
            if per == 1:
                most = jnp.max(s, axis=-1, keepdims=True)
            else:
                most = jnp.zeros_like(s)
                for slot in range(per):
                    here = lane_slot == slot
                    top = jnp.max(jnp.where(here, s, -jnp.inf), axis=-1, keepdims=True)
                    most = jnp.where(here, top, most)
            parts.append(jnp.exp((s - most) * scale).astype(jnp.bfloat16))
        weight = jnp.concatenate(parts, axis=1)
        weights.append(weight)
        mixed.append(jnp.dot(weight, spread_values, preferred_element_type=jnp.float32))
    weight = jnp.concatenate(weights, axis=0)
    total = jnp.dot(weight, ones_ref[...], preferred_element_type=jnp.float32)
    attended = (jnp.concatenate(mixed, axis=0) / total).astype(jnp.bfloat16)
    update = jnp.dot(attended, out_w, preferred_element_type=jnp.float32)
    return (rows + update).reshape(x.shape)


def enter(devices, me):
    barrier = pltpu.get_barrier_semaphore()

    @pl.loop(1, devices)
    def _(k):
        pl.semaphore_signal(
            barrier,
            inc=1,
            device_id={"mem": lax.rem(me + k, devices)},
            device_id_type=pl.DeviceIdType.MESH,
        )

    pl.semaphore_wait(barrier, devices - 1)


def exchange(source_of, target, me, devices, send_sem, recv_sem):
    own = pltpu.make_async_copy(source_of(me), target, recv_sem.at[me])
    own.start()

    @pl.loop(1, devices)
    def _(k):
        to = lax.rem(me + k, devices)
        pltpu.make_async_remote_copy(
            src_ref=source_of(to),
            dst_ref=target,
            send_sem=send_sem.at[to],
            recv_sem=recv_sem.at[me],
            device_id={"mem": to},
            device_id_type=pl.DeviceIdType.MESH,
        ).start()


def wait_all(ref, me, devices, sem, own):
    @pl.loop(0 if own else 1, devices)
    def _(k):
        pltpu.make_async_copy(ref, ref, sem.at[lax.rem(me + k, devices)]).wait()


def swap_strips(parts, width):
    count = len(parts)
    slot = lax.broadcasted_iota(jnp.int32, parts[0].shape, parts[0].ndim - 2) // width
    results = []
    for j in range(count):
        total = None
        for i in range(count):
            shift = ((i - j) * width) % (count * width)
            part = parts[i] if shift == 0 else pltpu.roll(parts[i], shift, parts[i].ndim - 2)
            total = part if total is None else jnp.where(slot == i, part, total)
        results.append(total)
    return results


def kernel(
    devices,
    x_ref,
    gain_ref,
    conv_hbm,
    qkv_ref,
    out_w_ref,
    out_ref,
    conv_ref,
    ones_ref,
    wide_ref,
    wide2_ref,
    state_ref,
    left_ref,
    right_ref,
    send_ref,
    recv_ref,
    send2_ref,
    recv2_ref,
    conv_sem,
    send_sem,
    recv_sem,
    send2_sem,
    recv2_sem,
    edge_send,
    edge_recv,
):
    members, rows, cols, channels = x_ref.shape
    width = cols // devices
    batch = 8 // width
    chunks = rows // batch
    groups = cols // 8
    everyone = members * devices
    pair = send_ref.shape[2]
    pair2 = send2_ref.shape[2]
    me = lax.axis_index("mem")
    flat = batch * cols
    column = lax.broadcasted_iota(jnp.int32, (flat, channels), 0) % cols
    loads = [
        pltpu.make_async_copy(conv_hbm.at[b], conv_ref.at[b], conv_sem.at[b]) for b in range(2)
    ]
    for load in loads:
        load.start()

    def fill(row):
        for member in range(members):
            x = x_ref[member, pl.ds(row, batch)].astype(jnp.float32).reshape(flat, channels)
            normed = normalised(x, gain_ref[0, 0:1])
            left = jnp.where(column == 0, 0.0, pltpu.roll(normed, 1, 0))
            right = jnp.where(column == cols - 1, 0.0, pltpu.roll(normed, flat - 1, 0))
            for at, value in enumerate((left, normed, right)):
                wide_ref[
                    member, pl.ds(row + 1, batch), :, at * channels : (at + 1) * channels
                ] = value.astype(jnp.bfloat16).reshape(batch, cols, channels)

    zero = jnp.zeros((members, 1, cols, 3 * channels), jnp.bfloat16)
    wide_ref[:, 0:1] = zero
    wide_ref[:, rows + 1 : rows + 2] = zero
    fill(0)
    enter(devices, me)
    loads[0].wait()

    @pl.loop(0, chunks)
    def _(q):
        row = q * batch

        @pl.when(q < chunks - 1)
        def _():
            fill(row + batch)

        total = taps(lambda di: wide_ref[:, pl.ds(row + di, batch)], conv_ref.at[0])
        x = x_ref[:, pl.ds(row, batch)].astype(jnp.float32).reshape(members * flat, channels)
        y = gated(x, total).reshape(members, batch, groups, 8, channels)
        parts = swap_strips(
            [y[:, i].reshape(members * groups, 8, channels) for i in range(batch)], width
        )
        for j in range(batch):
            part = parts[j].astype(jnp.bfloat16).reshape(members, groups, 8, channels)
            for k in range(groups):
                send_ref[q // pair, k * batch + j, q % pair] = part[:, k]

        @pl.when(q % pair == pair - 1)
        def _():
            g = q // pair
            exchange(
                lambda d: send_ref.at[g, d],
                recv_ref.at[g, me],
                me,
                devices,
                send_sem.at[g],
                recv_sem.at[g],
            )

    head_of_row = lax.broadcasted_iota(jnp.int32, ones_ref.shape, 0) // everyone
    head_of_lane = lax.broadcasted_iota(jnp.int32, ones_ref.shape, 1) // (channels // HEADS)
    ones_ref[...] = jnp.where(head_of_row == head_of_lane, 1.0, 0.0).astype(jnp.bfloat16)
    edge = jnp.zeros((1, width, everyone, 3 * channels), jnp.bfloat16)
    wide2_ref[0:1] = edge
    wide2_ref[rows + 1 : rows + 2] = edge

    @pl.when(me == 0)
    def _():
        left_ref[...] = jnp.zeros_like(left_ref)

    @pl.when(me == devices - 1)
    def _():
        right_ref[...] = jnp.zeros_like(right_ref)

    def to_right(q):
        span = pl.ds(q * batch, batch)
        return pltpu.make_async_remote_copy(
            src_ref=state_ref.at[span, width - 1],
            dst_ref=left_ref.at[span],
            send_sem=edge_send.at[0, q],
            recv_sem=edge_recv.at[0, q],
            device_id={"mem": lax.rem(me + 1, devices)},
            device_id_type=pl.DeviceIdType.MESH,
        )

    def to_left(q):
        span = pl.ds(q * batch, batch)
        return pltpu.make_async_remote_copy(
            src_ref=state_ref.at[span, 0],
            dst_ref=right_ref.at[span],
            send_sem=edge_send.at[1, q],
            recv_sem=edge_recv.at[1, q],
            device_id={"mem": lax.rem(me + devices - 1, devices)},
            device_id_type=pl.DeviceIdType.MESH,
        )

    def fill2(q):
        @pl.when(me > 0)
        def _():
            to_right(q).wait_recv()

        @pl.when(me < devices - 1)
        def _():
            to_left(q).wait_recv()

        for step in range(batch):
            row = q * batch + step
            for col in range(-1, width + 1):
                if col < 0:
                    x = left_ref[row]
                elif col == width:
                    x = right_ref[row]
                else:
                    x = state_ref[row, col]
                value = normalised(x.astype(jnp.float32), gain_ref[1, 0:1]).astype(jnp.bfloat16)
                for dj in range(3):
                    target = col + 1 - dj
                    if 0 <= target < width:
                        wide2_ref[row + 1, target, :, dj * channels : (dj + 1) * channels] = value

    @pl.loop(0, chunks + 2)
    def _(q):
        @pl.when(q < chunks)
        def _():
            g = q // pair

            @pl.when(q % pair == 0)
            def _():
                wait_all(recv_ref.at[g, 0], me, devices, recv_sem.at[g], True)

            x = recv_ref[g, :, q % pair].astype(jnp.float32).reshape(everyone, 8, channels)
            x = jnp.transpose(x, (1, 0, 2))
            y = attend_block(x, gain_ref[0, 1:2], qkv_ref[0], out_w_ref[0], ones_ref)
            y = y.astype(jnp.bfloat16).reshape(batch, width, everyone, channels)
            state_ref[pl.ds(q * batch, batch)] = y

            @pl.when(me < devices - 1)
            def _():
                to_right(q).start()

            @pl.when(me > 0)
            def _():
                to_left(q).start()

        @pl.when(q == 1)
        def _():
            loads[1].wait()

        @pl.when((q >= 1) & (q <= chunks))
        def _():
            fill2(q - 1)

        @pl.when(q >= 2)
        def _():
            p = q - 2
            row = p * batch
            total = taps(lambda di: wide2_ref[pl.ds(row + di, batch)], conv_ref.at[1])
            x = state_ref[pl.ds(row, batch)].astype(jnp.float32).reshape(-1, channels)
            x = gated(x, total).astype(jnp.bfloat16).astype(jnp.float32)
            x = x.reshape(8, everyone, channels)
            y = attend_block(x, gain_ref[1, 1:2], qkv_ref[1], out_w_ref[1], ones_ref)
            y = jnp.transpose(y, (1, 0, 2)).astype(jnp.bfloat16)
            g = p // pair2
            send2_ref[g, :, p % pair2] = y.reshape(devices, members, 8, channels)

            @pl.when(p % pair2 == pair2 - 1)
            def _():
                exchange(
                    lambda d: send2_ref.at[g, d],
                    recv2_ref.at[g, me],
                    me,
                    devices,
                    send2_sem.at[g],
                    recv2_sem.at[g],
                )

    @pl.loop(0, chunks // pair)
    def _(g):
        wait_all(send_ref.at[g, 0], me, devices, send_sem.at[g], False)

    @pl.loop(0, chunks)
    def _(q):
        @pl.when(me < devices - 1)
        def _():
            to_right(q).wait_send()

        @pl.when(me > 0)
        def _():
            to_left(q).wait_send()

    @pl.loop(0, chunks)
    def _(q):
        g = q // pair2

        @pl.when(q % pair2 == 0)
        def _():
            wait_all(recv2_ref.at[g, 0], me, devices, recv2_sem.at[g], True)

        parts = []
        for j in range(batch):
            part = [recv2_ref[g, k * batch + j, q % pair2].astype(jnp.float32) for k in range(groups)]
            parts.append(jnp.concatenate(part, axis=0))
        for i, part in enumerate(swap_strips(parts, width)):
            part = part.reshape(groups, members, 8, channels)
            for member in range(members):
                line = jnp.concatenate([part[k, member] for k in range(groups)], axis=0)
                out_ref[member, q * batch + i] = line.astype(jnp.bfloat16)

    @pl.loop(0, chunks // pair2)
    def _(g):
        wait_all(send2_ref.at[g, 0], me, devices, send2_sem.at[g], False)


def body(field, norm_gain, conv_weight, qkv_weight, out_weight):
    members, rows, cols, channels = field.shape
    devices = lax.axis_size("mem")
    width = cols // devices
    chunks = rows * width // 8
    everyone = members * devices
    vmem = lambda *shape: pltpu.VMEM(shape, jnp.bfloat16)
    pair, pair2 = math.gcd(OUTWARD, chunks), math.gcd(HOMEWARD, chunks)
    block = vmem(chunks // pair, devices, pair, members, 8, channels)
    block2 = vmem(chunks // pair2, devices, pair2, members, 8, channels)
    sems = pltpu.SemaphoreType.DMA((chunks // pair, devices))
    sems2 = pltpu.SemaphoreType.DMA((chunks // pair2, devices))
    edges = pltpu.SemaphoreType.DMA((2, chunks))
    here = pl.BlockSpec(memory_space=pltpu.VMEM)
    return pl.pallas_call(
        functools.partial(kernel, devices),
        in_specs=[here, here, pl.BlockSpec(memory_space=pl.ANY), here, here],
        out_specs=here,
        out_shape=jax.ShapeDtypeStruct(field.shape, jnp.bfloat16),
        scratch_shapes=[
            vmem(*conv_weight.shape),
            vmem(HEADS * everyone, channels),
            vmem(members, rows + 2, cols, 3 * channels),
            vmem(rows + 2, width, everyone, 3 * channels),
            vmem(rows, width, everyone, channels),
            vmem(rows, everyone, channels),
            vmem(rows, everyone, channels),
            block,
            block,
            block2,
            block2,
            pltpu.SemaphoreType.DMA((2,)),
            sems,
            sems,
            sems2,
            sems2,
            edges,
            edges,
        ],
        compiler_params=pltpu.CompilerParams(
            vmem_limit_bytes=VMEM_LIMIT, collective_id=0, has_side_effects=True
        ),
        name="transformer",
    )(field, norm_gain, conv_weight, qkv_weight, out_weight)


def solution(mesh):
    return jax.shard_map(
        body,
        mesh=mesh,
        in_specs=(P(("grp", "mem"), None, None, None), P(), P(), P(), P()),
        out_specs=P(("grp", "mem"), None, None, None),
        check_vma=False,
    )
```

```python
import functools
import math

import jax
import jax.numpy as jnp
from jax import lax
from jax.experimental import pallas as pl
from jax.experimental.pallas import tpu as pltpu
from jax.sharding import PartitionSpec as P

HEADS = 8
epsilon = 1e-06
OUTWARD = 2
HOMEWARD = 2
VMEM_LIMIT = 58 * 1024 * 1024


def normalised(x, gain):
    inverse = lax.rsqrt(jnp.mean(x * x, axis=-1, keepdims=True) + epsilon)
    return x * inverse * gain


def gated(x, conv_out):
    channels = x.shape[-1]
    gate = conv_out[:, channels:]
    return x + conv_out[:, :channels] * (1.0 / (1.0 + jnp.exp(-gate)))


def taps(rows_of, weight_ref):
    total = None
    for di in range(3):
        lhs = rows_of(di)
        lhs = lhs.reshape(-1, lhs.shape[-1])
        weight = weight_ref[di].reshape(lhs.shape[-1], -1)
        part = jnp.dot(lhs, weight, preferred_element_type=jnp.float32)
        total = part if total is None else total + part
    return total


def attend_block(x, gain, qkv, out_w, ones_ref):
    cells, members, channels = x.shape
    head_size = channels // HEADS
    scale = head_size ** (-0.5)
    rows = x.reshape(cells * members, channels)
    normed = normalised(rows, gain).astype(jnp.bfloat16)
    projected = jnp.dot(normed, qkv, preferred_element_type=jnp.float32).astype(
        jnp.bfloat16
    )
    lane_head = lax.broadcasted_iota(jnp.int32, (members, channels), 1) // head_size
    masks = [lane_head == h for h in range(HEADS)]
    zero = jnp.zeros((members, channels), jnp.bfloat16)
    per = max(1, 128 // members)
    width = per * members
    lane_slot = lax.broadcasted_iota(jnp.int32, (members, width), 1) // members
    weights, mixed = [], []
    for cell in range(cells):
        block = projected[cell * members : (cell + 1) * members]
        queries = block[:, :channels]
        keys = block[:, channels : 2 * channels]
        values = block[:, 2 * channels :]
        spread_keys = jnp.concatenate([jnp.where(m, keys, zero) for m in masks], axis=0)
        spread_values = jnp.concatenate([jnp.where(m, values, zero) for m in masks], axis=0)
        scores = lax.dot_general(
            queries, spread_keys, (((1,), (1,)), ((), ())), preferred_element_type=jnp.float32
        )
        parts = []
        for tile in range(HEADS // per):
            s = scores[:, tile * width : (tile + 1) * width]
            if per == 1:
                most = jnp.max(s, axis=-1, keepdims=True)
            else:
                most = jnp.zeros_like(s)
                for slot in range(per):
                    here = lane_slot == slot
                    top = jnp.max(jnp.where(here, s, -jnp.inf), axis=-1, keepdims=True)
                    most = jnp.where(here, top, most)
            parts.append(jnp.exp((s - most) * scale).astype(jnp.bfloat16))
        weight = jnp.concatenate(parts, axis=1)
        weights.append(weight)
        mixed.append(jnp.dot(weight, spread_values, preferred_element_type=jnp.float32))
    weight = jnp.concatenate(weights, axis=0)
    total = jnp.dot(weight, ones_ref[...], preferred_element_type=jnp.float32)
    attended = (jnp.concatenate(mixed, axis=0) / total).astype(jnp.bfloat16)
    update = jnp.dot(attended, out_w, preferred_element_type=jnp.float32)
    return (rows + update).reshape(x.shape)


def enter(devices, me):
    barrier = pltpu.get_barrier_semaphore()

    @pl.loop(1, devices)
    def _(k):
        pl.semaphore_signal(
            barrier,
            inc=1,
            device_id={"mem": lax.rem(me + k, devices)},
            device_id_type=pl.DeviceIdType.MESH,
        )

    pl.semaphore_wait(barrier, devices - 1)


def exchange(source_of, target, me, devices, send_sem, recv_sem):
    own = pltpu.make_async_copy(source_of(me), target, recv_sem.at[me])
    own.start()

    @pl.loop(1, devices)
    def _(k):
        to = lax.rem(me + k, devices)
        pltpu.make_async_remote_copy(
            src_ref=source_of(to),
            dst_ref=target,
            send_sem=send_sem.at[to],
            recv_sem=recv_sem.at[me],
            device_id={"mem": to},
            device_id_type=pl.DeviceIdType.MESH,
        ).start()


def wait_all(ref, me, devices, sem, own):
    @pl.loop(0 if own else 1, devices)
    def _(k):
        pltpu.make_async_copy(ref, ref, sem.at[lax.rem(me + k, devices)]).wait()


def swap_strips(parts, width):
    count = len(parts)
    slot = lax.broadcasted_iota(jnp.int32, parts[0].shape, parts[0].ndim - 2) // width
    results = []
    for j in range(count):
        total = None
        for i in range(count):
            shift = ((i - j) * width) % (count * width)
            part = parts[i] if shift == 0 else pltpu.roll(parts[i], shift, parts[i].ndim - 2)
            total = part if total is None else jnp.where(slot == i, part, total)
        results.append(total)
    return results


def kernel(
    devices,
    x_ref,
    gain_ref,
    conv_hbm,
    qkv_ref,
    out_w_ref,
    out_ref,
    conv_ref,
    ones_ref,
    wide_ref,
    wide2_ref,
    state_ref,
    left_ref,
    right_ref,
    send_ref,
    recv_ref,
    send2_ref,
    recv2_ref,
    conv_sem,
    send_sem,
    recv_sem,
    send2_sem,
    recv2_sem,
    edge_send,
    edge_recv,
):
    members, rows, cols, channels = x_ref.shape
    width = cols // devices
    batch = 8 // width
    chunks = rows // batch
    groups = cols // 8
    everyone = members * devices
    pair = send_ref.shape[2]
    pair2 = send2_ref.shape[2]
    me = lax.axis_index("mem")
    flat = batch * cols
    column = lax.broadcasted_iota(jnp.int32, (flat, channels), 0) % cols
    loads = [
        pltpu.make_async_copy(conv_hbm.at[b], conv_ref.at[b], conv_sem.at[b]) for b in range(2)
    ]
    for load in loads:
        load.start()

    def fill(row):
        for member in range(members):
            x = x_ref[member, pl.ds(row, batch)].astype(jnp.float32).reshape(flat, channels)
            normed = normalised(x, gain_ref[0, 0:1])
            left = jnp.where(column == 0, 0.0, pltpu.roll(normed, 1, 0))
            right = jnp.where(column == cols - 1, 0.0, pltpu.roll(normed, flat - 1, 0))
            for at, value in enumerate((left, normed, right)):
                wide_ref[
                    member, pl.ds(row + 1, batch), :, at * channels : (at + 1) * channels
                ] = value.astype(jnp.bfloat16).reshape(batch, cols, channels)

    zero = jnp.zeros((members, 1, cols, 3 * channels), jnp.bfloat16)
    wide_ref[:, 0:1] = zero
    wide_ref[:, rows + 1 : rows + 2] = zero
    fill(0)
    enter(devices, me)
    loads[0].wait()

    @pl.loop(0, chunks)
    def _(q):
        row = q * batch

        @pl.when(q < chunks - 1)
        def _():
            fill(row + batch)

        total = taps(lambda di: wide_ref[:, pl.ds(row + di, batch)], conv_ref.at[0])
        x = x_ref[:, pl.ds(row, batch)].astype(jnp.float32).reshape(members * flat, channels)
        y = gated(x, total).reshape(members, batch, groups, 8, channels)
        parts = swap_strips(
            [y[:, i].reshape(members * groups, 8, channels) for i in range(batch)], width
        )
        for j in range(batch):
            part = parts[j].astype(jnp.bfloat16).reshape(members, groups, 8, channels)
            for k in range(groups):
                send_ref[q // pair, k * batch + j, q % pair] = part[:, k]

        @pl.when(q % pair == pair - 1)
        def _():
            g = q // pair
            exchange(
                lambda d: send_ref.at[g, d],
                recv_ref.at[g, me],
                me,
                devices,
                send_sem.at[g],
                recv_sem.at[g],
            )

    head_of_row = lax.broadcasted_iota(jnp.int32, ones_ref.shape, 0) // everyone
    head_of_lane = lax.broadcasted_iota(jnp.int32, ones_ref.shape, 1) // (channels // HEADS)
    ones_ref[...] = jnp.where(head_of_row == head_of_lane, 1.0, 0.0).astype(jnp.bfloat16)
    edge = jnp.zeros((1, width, everyone, 3 * channels), jnp.bfloat16)
    wide2_ref[0:1] = edge
    wide2_ref[rows + 1 : rows + 2] = edge

    @pl.when(me == 0)
    def _():
        left_ref[...] = jnp.zeros_like(left_ref)

    @pl.when(me == devices - 1)
    def _():
        right_ref[...] = jnp.zeros_like(right_ref)

    def to_right(q):
        span = pl.ds(q * batch, batch)
        return pltpu.make_async_remote_copy(
            src_ref=state_ref.at[span, width - 1],
            dst_ref=left_ref.at[span],
            send_sem=edge_send.at[0, q],
            recv_sem=edge_recv.at[0, q],
            device_id={"mem": lax.rem(me + 1, devices)},
            device_id_type=pl.DeviceIdType.MESH,
        )

    def to_left(q):
        span = pl.ds(q * batch, batch)
        return pltpu.make_async_remote_copy(
            src_ref=state_ref.at[span, 0],
            dst_ref=right_ref.at[span],
            send_sem=edge_send.at[1, q],
            recv_sem=edge_recv.at[1, q],
            device_id={"mem": lax.rem(me + devices - 1, devices)},
            device_id_type=pl.DeviceIdType.MESH,
        )

    def fill2(q):
        @pl.when(me > 0)
        def _():
            to_right(q).wait_recv()

        @pl.when(me < devices - 1)
        def _():
            to_left(q).wait_recv()

        for step in range(batch):
            row = q * batch + step
            for col in range(-1, width + 1):
                if col < 0:
                    x = left_ref[row]
                elif col == width:
                    x = right_ref[row]
                else:
                    x = state_ref[row, col]
                value = normalised(x.astype(jnp.float32), gain_ref[1, 0:1]).astype(jnp.bfloat16)
                for dj in range(3):
                    target = col + 1 - dj
                    if 0 <= target < width:
                        wide2_ref[row + 1, target, :, dj * channels : (dj + 1) * channels] = value

    @pl.loop(0, chunks + 2)
    def _(q):
        @pl.when(q == 1)
        def _():
            loads[1].wait()

        @pl.when((q >= 1) & (q <= chunks))
        def _():
            fill2(q - 1)

        @pl.when(q >= 2)
        def _():
            p = q - 2
            row = p * batch
            total = taps(lambda di: wide2_ref[pl.ds(row + di, batch)], conv_ref.at[1])
            x = state_ref[pl.ds(row, batch)].astype(jnp.float32).reshape(-1, channels)
            x = gated(x, total).astype(jnp.bfloat16).astype(jnp.float32)
            x = x.reshape(8, everyone, channels)
            y = attend_block(x, gain_ref[1, 1:2], qkv_ref[1], out_w_ref[1], ones_ref)
            y = jnp.transpose(y, (1, 0, 2)).astype(jnp.bfloat16)
            g = p // pair2
            send2_ref[g, :, p % pair2] = y.reshape(devices, members, 8, channels)

            @pl.when(p % pair2 == pair2 - 1)
            def _():
                exchange(
                    lambda d: send2_ref.at[g, d],
                    recv2_ref.at[g, me],
                    me,
                    devices,
                    send2_sem.at[g],
                    recv2_sem.at[g],
                )

        @pl.when(q < chunks)
        def _():
            g = q // pair

            @pl.when(q % pair == 0)
            def _():
                wait_all(recv_ref.at[g, 0], me, devices, recv_sem.at[g], True)

            x = recv_ref[g, :, q % pair].astype(jnp.float32).reshape(everyone, 8, channels)
            x = jnp.transpose(x, (1, 0, 2))
            y = attend_block(x, gain_ref[0, 1:2], qkv_ref[0], out_w_ref[0], ones_ref)
            y = y.astype(jnp.bfloat16).reshape(batch, width, everyone, channels)
            state_ref[pl.ds(q * batch, batch)] = y

            @pl.when(me < devices - 1)
            def _():
                to_right(q).start()

            @pl.when(me > 0)
            def _():
                to_left(q).start()

    @pl.loop(0, chunks // pair)
    def _(g):
        wait_all(send_ref.at[g, 0], me, devices, send_sem.at[g], False)

    @pl.loop(0, chunks)
    def _(q):
        @pl.when(me < devices - 1)
        def _():
            to_right(q).wait_send()

        @pl.when(me > 0)
        def _():
            to_left(q).wait_send()

    @pl.loop(0, chunks)
    def _(q):
        g = q // pair2

        @pl.when(q % pair2 == 0)
        def _():
            wait_all(recv2_ref.at[g, 0], me, devices, recv2_sem.at[g], True)

        parts = []
        for j in range(batch):
            part = [recv2_ref[g, k * batch + j, q % pair2].astype(jnp.float32) for k in range(groups)]
            parts.append(jnp.concatenate(part, axis=0))
        for i, part in enumerate(swap_strips(parts, width)):
            part = part.reshape(groups, members, 8, channels)
            for member in range(members):
                line = jnp.concatenate([part[k, member] for k in range(groups)], axis=0)
                out_ref[member, q * batch + i] = line.astype(jnp.bfloat16)

    @pl.loop(0, chunks // pair2)
    def _(g):
        wait_all(send2_ref.at[g, 0], me, devices, send2_sem.at[g], False)


def body(field, norm_gain, conv_weight, qkv_weight, out_weight):
    members, rows, cols, channels = field.shape
    devices = lax.axis_size("mem")
    width = cols // devices
    chunks = rows * width // 8
    everyone = members * devices
    vmem = lambda *shape: pltpu.VMEM(shape, jnp.bfloat16)
    pair, pair2 = math.gcd(OUTWARD, chunks), math.gcd(HOMEWARD, chunks)
    block = vmem(chunks // pair, devices, pair, members, 8, channels)
    block2 = vmem(chunks // pair2, devices, pair2, members, 8, channels)
    sems = pltpu.SemaphoreType.DMA((chunks // pair, devices))
    sems2 = pltpu.SemaphoreType.DMA((chunks // pair2, devices))
    edges = pltpu.SemaphoreType.DMA((2, chunks))
    here = pl.BlockSpec(memory_space=pltpu.VMEM)
    return pl.pallas_call(
        functools.partial(kernel, devices),
        in_specs=[here, here, pl.BlockSpec(memory_space=pl.ANY), here, here],
        out_specs=here,
        out_shape=jax.ShapeDtypeStruct(field.shape, jnp.bfloat16),
        scratch_shapes=[
            vmem(*conv_weight.shape),
            vmem(HEADS * everyone, channels),
            vmem(members, rows + 2, cols, 3 * channels),
            vmem(rows + 2, width, everyone, 3 * channels),
            vmem(rows, width, everyone, channels),
            vmem(rows, everyone, channels),
            vmem(rows, everyone, channels),
            block,
            block,
            block2,
            block2,
            pltpu.SemaphoreType.DMA((2,)),
            sems,
            sems,
            sems2,
            sems2,
            edges,
            edges,
        ],
        compiler_params=pltpu.CompilerParams(
            vmem_limit_bytes=VMEM_LIMIT, collective_id=0, has_side_effects=True
        ),
        name="transformer",
    )(field, norm_gain, conv_weight, qkv_weight, out_weight)


def solution(mesh):
    return jax.shard_map(
        body,
        mesh=mesh,
        in_specs=(P(("grp", "mem"), None, None, None), P(), P(), P(), P()),
        out_specs=P(("grp", "mem"), None, None, None),
        check_vma=False,
    )
```
